128 devices in a mesh: wide: 16 (over z, y_hi, core), narrow: 8 (over y_lo, x).
Axes of the slice: x: 4, y: 4 (y_hi: 2, y_lo: 2; y = y_hi * 2 + y_lo), z: 4, core: 2. Of those that a mesh axis runs over, the one named last changes fastest.
Arguments:
- cholesky: bfloat16 [2048, 262144], P('narrow', 'wide'), may hold values from -0.015625 to 0.015625
- fields: bfloat16 [2, 128, 2048], P(None, 'wide', 'narrow'), may hold values from -4 to 4
- walkers: bfloat16 [128, 512, 128], P(('wide', 'narrow')), may hold values from -5 to 5
- one_body: bfloat16 [512, 512], replicated, may hold values from -0.078125 to 1
Outputs:
- propagated: bfloat16 [128, 512, 128], P(('wide', 'narrow'))
The draws below stay inside these ranges and needn't reach their ends.
All inputs are finite; a program needn't handle non-finite values.
Results may differ from the reference program's by a relative error of at most 0.024.
Values may be sent and summed in bfloat16 or wider, within the bound.
No kernel may reach another device: no remote copies, remote signals or barrier semaphores. Data moves between devices by JAX's collectives and lax.ppermute only.
A program may use at most 128 MiB of HBM per device.

```python
import jax
import jax.numpy as jnp
from jax import lax

NORB = 512
NE = 64
NCHOL = 2048
STEPS = 2
ORDER = 6
WALKERS = 128
CHOL_DEV = 256
N_NARROW = 8


def draw_one_body(key, part):
    key_off, key_diag = jax.random.split(jax.random.fold_in(key, 17), 2)
    spread = 0.2
    lowest = 0.7
    entries = jax.random.normal(key_off, (NORB, NORB), jnp.float32)
    symmetric = (entries + entries.T) * (spread / (2.0 * NORB) ** 0.5)
    symmetric = jnp.clip(symmetric, -0.078125, 0.078125)
    diagonal = jax.random.uniform(key_diag, (NORB,), jnp.float32, lowest, 1.0)
    identity = jnp.eye(NORB, dtype=jnp.float32)
    return (symmetric * (1.0 - identity) + identity * diagonal[:, None]).astype(jnp.bfloat16)


def block_scale(stream_key, shape, cuts, least, largest):
    def one(dim, parts):
        draws = jax.random.uniform(jax.random.fold_in(jax.random.fold_in(stream_key, 6), dim), (parts,), jnp.float32, least / len(cuts), largest / len(cuts))
        return jnp.repeat(jnp.exp(draws), shape[dim] // parts).reshape((-1,) + (1,) * (len(shape) - dim - 1))

    gain = one(*cuts[0])
    for cut in cuts[1:]:
        gain = gain * one(*cut)
    return gain


def noise(stream_key, extent, scale, bound, cuts=(), kind=jnp.bfloat16):
    array = jax.random.normal(stream_key, extent, jnp.float32) * scale
    if len(cuts) > 0:
        array = block_scale(stream_key, extent, cuts, -0.22, 0.18) * array
    return jnp.clip(array, min=-bound, max=bound).astype(kind)


def setup_inputs(seed: int = 0) -> dict:
    seeds = jax.random.split(jax.random.key(seed), 5)
    cholesky = noise(seeds[0], (NCHOL, NORB * NORB), (1.06 / (NORB * NCHOL) ** 0.5), 0.015625, ((0, 8), (1, 16)))
    fields = noise(seeds[1], (STEPS, WALKERS, NCHOL), 1.0, 4.0, ((1, 16), (2, 8)))
    walkers = noise(seeds[2], (WALKERS, NORB, 2 * NE), 1.0, 5.0, ((0, 128),))
    one_body = draw_one_body(jax.random.fold_in(seeds[4], 71), 0)
    return {"cholesky": cholesky, "fields": fields, "walkers": walkers, "one_body": one_body}


def taylor_apply(propagator, walker, one_body):
    half_cols = walker.shape[1] // 2
    term_now = walker
    summed = walker.astype(jnp.float32)
    for order_index in range(1, ORDER + 1):
        direct_part = jnp.dot(propagator, term_now, preferred_element_type=jnp.float32)
        mirror_part = jnp.dot(propagator.T, term_now, preferred_element_type=jnp.float32)
        product = (direct_part + mirror_part) / order_index
        rotated = jnp.concatenate((-product[:, half_cols:], product[:, :half_cols]), axis=1)
        summed = summed + rotated
        term_now = rotated.astype(jnp.bfloat16)
    stepped = summed.astype(jnp.bfloat16)
    return jnp.dot(one_body, stepped, preferred_element_type=jnp.float32).astype(jnp.bfloat16)


def reference(cholesky, fields, walkers, one_body):
    current = walkers
    for step_index in range(STEPS):
        field_now = fields[step_index]
        summed = jnp.zeros((WALKERS, NORB * NORB), jnp.float32)
        for block_index in range(N_NARROW):
            lower_row = block_index * CHOL_DEV
            partial_value = jnp.dot(field_now[:, lower_row:lower_row + CHOL_DEV], cholesky[lower_row:lower_row + CHOL_DEV], preferred_element_type=jnp.float32)
            partial_value = lax.optimization_barrier(partial_value.astype(jnp.bfloat16))
            summed = summed + partial_value.astype(jnp.float32)
        propagator = summed.astype(jnp.bfloat16).reshape(WALKERS, NORB, NORB)

        def advance(operands):
            matrix_in, walker = operands
            return taylor_apply(matrix_in, walker, one_body)

        current = lax.map(advance, (propagator, current))
    return current
```

```python
import jax
import jax.numpy as jnp
from jax import lax
from jax.experimental import pallas as pl
from jax.experimental.pallas import tpu as pltpu
from jax.sharding import PartitionSpec as P

ORDER = 6

LINK = {"A": 1, "B": 3, "C": 4}
ORDERS = ("ABC", "BCA", "CAB")
TILES = 8
UNITS = ((6, 5, 5), (5, 5, 6))


def widths(step):
    return tuple(128 * u for u in UNITS[step])


def arranged(fields_all, me, order, step, rows):
    row = lax.broadcasted_iota(jnp.int32, (rows, 256), 0)
    col = lax.broadcasted_iota(jnp.int32, (rows, 256), 1)
    slot = row // 16
    group = row % 16
    relative = ((slot // 4) % 2) * LINK[order[0]]
    relative = relative ^ (((slot // 2) % 2) * LINK[order[1]])
    relative = relative ^ ((slot % 2) * LINK[order[2]])
    source = group * 16 + step * 8 + (relative ^ me)
    pick = jnp.where(col == source, 1.0, 0.0).astype(jnp.bfloat16)
    return jnp.dot(pick, fields_all, preferred_element_type=jnp.float32).astype(jnp.bfloat16)


def partial_kernel(step, me_ref, fields_ref, chol_ref, *rest):
    outs, picked = rest[:6], rest[6]

    @pl.when(pl.program_id(0) == 0)
    def _():
        for part in range(3):
            picked[part] = arranged(fields_ref[...], me_ref[0], ORDERS[part], step, 128)

    start = 0
    for part, width in enumerate(widths(step)):
        value = jnp.dot(
            picked[part], chol_ref[:, start : start + width], preferred_element_type=jnp.float32
        ).astype(jnp.bfloat16)
        outs[2 * part][...] = value[:64]
        outs[2 * part + 1][...] = value[64:]
        start += width


def partials(step, me, fields_all, cholesky):
    out_shape, out_specs = [], []
    for width in widths(step):
        for _ in range(2):
            out_shape.append(jax.ShapeDtypeStruct((64, width * TILES), jnp.bfloat16))
            out_specs.append(pl.BlockSpec((64, width), lambda i, me: (0, i)))
    return pl.pallas_call(
        lambda *refs: partial_kernel(step, *refs),
        grid_spec=pltpu.PrefetchScalarGridSpec(
            num_scalar_prefetch=1,
            grid=(TILES,),
            in_specs=[
                pl.BlockSpec((256, 256), lambda i, me: (0, 0)),
                pl.BlockSpec((256, 2048), lambda i, me: (0, i)),
            ],
            out_specs=out_specs,
            scratch_shapes=[pltpu.VMEM((3, 128, 256), jnp.bfloat16)],
        ),
        out_shape=out_shape,
        cost_estimate=pl.CostEstimate(
            flops=2 * 128 * 256 * 16384, bytes_accessed=12 << 20, transcendentals=0
        ),
        name=f"partials{step}",
    )(me, fields_all, cholesky)


def swap(value, link):
    bit = LINK[link]
    return lax.ppermute(value, "narrow", [(i, i ^ bit) for i in range(8)])


def plus(a, b):
    return (a.astype(jnp.float32) + b.astype(jnp.float32)).astype(jnp.bfloat16)


def tiles_kernel(step, *refs):
    ins, out_ref, scratch = refs[:6], refs[6], refs[7]
    w = widths(step)
    for tile in range(TILES):
        pieces = []
        for part in range(3):
            cols = slice(tile * w[part], (tile + 1) * w[part])
            pieces.append(
                ins[2 * part][:, cols].astype(jnp.float32)
                + ins[2 * part + 1][:, cols].astype(jnp.float32)
            )
        whole = jnp.concatenate(pieces, axis=1)
        for row in range(4):
            for lane in range(4):
                first = row * 512 + lane * 128
                scratch[lane, pl.ds(tile * 4 + row, 16, stride=32), :] = whole[:, first : first + 128]
    for lane in range(4):
        out_ref[:, :, lane * 128 : (lane + 1) * 128] = (
            scratch[lane].astype(jnp.bfloat16).reshape(16, 32, 128)
        )


def owner_tiles(step, pairs):
    flat = [x for pair in pairs for x in pair]
    return pl.pallas_call(
        lambda *refs: tiles_kernel(step, *refs),
        out_shape=jax.ShapeDtypeStruct((16, 32, 512), jnp.bfloat16),
        scratch_shapes=[pltpu.VMEM((4, 512, 128), jnp.float32)],
        cost_estimate=pl.CostEstimate(flops=1 << 20, bytes_accessed=3 << 19, transcendentals=0),
        name=f"tiles{step}",
    )(*flat)


def taylor_kernel(prop_ref, walker_ref, one_body_ref, out_ref):
    prop = prop_ref[...].astype(jnp.float32)
    both = (prop + prop.T).astype(jnp.bfloat16)
    term = walker_ref[...]
    even = term.astype(jnp.float32)
    odd = jnp.zeros_like(even)
    for k in range(1, ORDER + 1):
        grown = jnp.dot(both, term, preferred_element_type=jnp.float32) * (1.0 / k)
        if k % 2:
            odd = odd + grown if k % 4 == 1 else odd - grown
        else:
            even = even + grown if k % 4 == 0 else even - grown
        term = grown.astype(jnp.bfloat16)
    half = even.shape[1] // 2
    turned = jnp.concatenate((-odd[:, half:], odd[:, :half]), axis=1)
    stepped = (even + turned).astype(jnp.bfloat16)
    out_ref[...] = jnp.dot(
        one_body_ref[...], stepped, preferred_element_type=jnp.float32
    ).astype(jnp.bfloat16)


def taylor(step, prop, walker, one_body):
    return pl.pallas_call(
        taylor_kernel,
        out_shape=jax.ShapeDtypeStruct(walker.shape, jnp.bfloat16),
        cost_estimate=pl.CostEstimate(
            flops=2 * 7 * 512 * 512 * 128, bytes_accessed=3 << 19, transcendentals=0
        ),
        name=f"taylor{step}",
    )(prop, walker, one_body)


def gather_fields(fields):
    spread = jnp.broadcast_to(fields[None], (16,) + fields.shape)
    every = lax.all_to_all(spread, "wide", split_axis=0, concat_axis=0, tiled=True)
    return every.reshape(256, 256)


def local(cholesky, fields, walkers, one_body):
    me = lax.axis_index("narrow").astype(jnp.int32).reshape(1)
    fields_all = gather_fields(fields)
    steps = (0, 1)
    keep, sent = {}, {}
    for s in steps:
        out = partials(s, me, fields_all, cholesky)
        keep[s] = [out[2 * p] for p in range(3)]
        sent[s] = [swap(out[2 * p + 1], ORDERS[p][0]) for p in range(3)]
    for stage, rows in ((1, 32), (2, 16)):
        for s in steps:
            send = [plus(keep[s][p][rows:], sent[s][p][rows:]) for p in range(3)]
            keep[s] = [plus(keep[s][p][:rows], sent[s][p][:rows]) for p in range(3)]
            sent[s] = [swap(send[p], ORDERS[p][stage]) for p in range(3)]
    current = walkers.reshape(512, 128)
    for s in steps:
        tiles = owner_tiles(s, list(zip(keep[s], sent[s])))
        prop = lax.all_to_all(tiles, "wide", split_axis=0, concat_axis=0, tiled=True)
        current = taylor(s, prop.reshape(512, 512), current, one_body)
    return current.reshape(walkers.shape)


def solution(mesh):
    return jax.shard_map(
        local,
        mesh=mesh,
        in_specs=(
            P("narrow", "wide"),
            P(None, "wide", "narrow"),
            P(("wide", "narrow"), None, None),
            P(),
        ),
        out_specs=P(("wide", "narrow"), None, None),
        check_vma=False,
    )
```

```python
import jax
import jax.numpy as jnp
from jax import lax
from jax.experimental import pallas as pl
from jax.experimental.pallas import tpu as pltpu
from jax.sharding import PartitionSpec as P

ORDER = 6

LINK = {"A": 1, "B": 3, "C": 4}
ORDERS = ("ABC", "BCA", "CAB")
BOUNDS = (0, 43 * 128, 86 * 128, 128 * 128)
CHUNK = 1024
SMALL = pltpu.CompilerParams(vmem_limit_bytes=16 << 20)
TINY = pltpu.CompilerParams(vmem_limit_bytes=8 << 20)
VMEM = pl.BlockSpec(memory_space=pltpu.VMEM)


def arranged(fields_all, me, order):
    row = lax.broadcasted_iota(jnp.int32, (256, 256), 0)
    col = lax.broadcasted_iota(jnp.int32, (256, 256), 1)
    group, last, middle = row % 16, (row // 16) % 2, (row // 32) % 2
    step, first = (row // 64) % 2, row // 128
    relative = (first * LINK[order[0]]) ^ (middle * LINK[order[1]]) ^ (last * LINK[order[2]])
    source = group * 16 + step * 8 + (relative ^ me)
    pick = jnp.where(col == source, 1.0, 0.0).astype(jnp.bfloat16)
    return jnp.dot(pick, fields_all, preferred_element_type=jnp.float32).astype(jnp.bfloat16)


def partial_kernel(part, me_ref, fields_ref, chol_ref, *rest):
    outs, loaded, sems = rest[:4], rest[4], rest[5]
    first, last = BOUNDS[part], BOUNDS[part + 1]
    spans = [(low, min(low + CHUNK, last)) for low in range(first, last, CHUNK)]
    copies = []
    for index, (low, high) in enumerate(spans):
        copies.append(
            pltpu.make_async_copy(
                chol_ref.at[:, low:high], loaded.at[:, low - first : high - first], sems.at[index]
            )
        )
        copies[-1].start()
    picked = arranged(fields_ref[...], me_ref[0], ORDERS[part])
    for copy, (low, high) in zip(copies, spans):
        copy.wait()
        value = jnp.dot(
            picked, loaded[:, low - first : high - first], preferred_element_type=jnp.float32
        ).astype(jnp.bfloat16)
        for out in range(4):
            outs[out][:, low - first : high - first] = value[64 * out : 64 * out + 64]


def partials(part, me, fields_all, cholesky):
    width = BOUNDS[part + 1] - BOUNDS[part]
    return pl.pallas_call(
        lambda *refs: partial_kernel(part, *refs),
        in_specs=[
            pl.BlockSpec(memory_space=pltpu.SMEM),
            VMEM,
            pl.BlockSpec(memory_space=pl.ANY),
        ],
        out_specs=[VMEM] * 4,
        out_shape=[pltpu.VMEM((64, width), jnp.bfloat16)] * 4,
        scratch_shapes=[
            pltpu.VMEM((256, width), jnp.bfloat16),
            pltpu.SemaphoreType.DMA((pl.cdiv(width, CHUNK),)),
        ],
        compiler_params=SMALL,
        cost_estimate=pl.CostEstimate(
            flops=2 * 256 * 256 * width, bytes_accessed=4 << 20, transcendentals=0
        ),
        name=f"partials{part}",
    )(me, fields_all, cholesky)


def swap(value, link):
    bit = LINK[link]
    return lax.ppermute(value, "narrow", [(i, i ^ bit) for i in range(8)])


def plus(a, b):
    return (a.astype(jnp.float32) + b.astype(jnp.float32)).astype(jnp.bfloat16)


def tiles_kernel(*refs):
    ins, out_ref, scratch = refs[:6], refs[6], refs[7]
    for row in range(32):
        for part in range(3):
            low = max(row * 512, BOUNDS[part])
            high = min(row * 512 + 512, BOUNDS[part + 1])
            if low < high:
                cols = slice(low - BOUNDS[part], high - BOUNDS[part])
                total = ins[2 * part][:, cols].astype(jnp.float32) + ins[2 * part + 1][
                    :, cols
                ].astype(jnp.float32)
                scratch[row * 16 : row * 16 + 16, low - row * 512 : high - row * 512] = (
                    total.astype(jnp.bfloat16)
                )
    row = lax.broadcasted_iota(jnp.int32, (512, 512), 0)
    col = lax.broadcasted_iota(jnp.int32, (512, 512), 1)
    turn = jnp.where((row % 32) * 16 + row // 32 == col, 1.0, 0.0).astype(jnp.bfloat16)
    out_ref[...] = (
        jnp.dot(turn, scratch[...], preferred_element_type=jnp.float32)
        .astype(jnp.bfloat16)
        .reshape(16, 32, 512)
    )


def owner_tiles(step, pairs):
    flat = [x for pair in pairs for x in pair]
    return pl.pallas_call(
        tiles_kernel,
        in_specs=[VMEM] * 6,
        out_specs=VMEM,
        out_shape=pltpu.VMEM((16, 32, 512), jnp.bfloat16),
        scratch_shapes=[pltpu.VMEM((512, 512), jnp.bfloat16)],
        compiler_params=TINY,
        cost_estimate=pl.CostEstimate(flops=1 << 28, bytes_accessed=3 << 19, transcendentals=0),
        name=f"tiles{step}",
    )(*flat)


def taylor_kernel(prop_ref, walker_ref, one_body_ref, out_ref):
    prop = prop_ref[...].astype(jnp.float32)
    both = (prop + prop.T).astype(jnp.bfloat16)
    term = walker_ref[...]
    even = term.astype(jnp.float32)
    odd = jnp.zeros_like(even)
    for k in range(1, ORDER + 1):
        grown = jnp.dot(both, term, preferred_element_type=jnp.float32) * (1.0 / k)
        if k % 2:
            odd = odd + grown if k % 4 == 1 else odd - grown
        else:
            even = even + grown if k % 4 == 0 else even - grown
        term = grown.astype(jnp.bfloat16)
    half = even.shape[1] // 2
    turned = jnp.concatenate((-odd[:, half:], odd[:, :half]), axis=1)
    stepped = (even + turned).astype(jnp.bfloat16)
    out_ref[...] = jnp.dot(
        one_body_ref[...], stepped, preferred_element_type=jnp.float32
    ).astype(jnp.bfloat16)


def taylor(step, prop, walker, one_body):
    return pl.pallas_call(
        taylor_kernel,
        in_specs=[VMEM] * 3,
        out_specs=VMEM,
        out_shape=jax.ShapeDtypeStruct(walker.shape, jnp.bfloat16),
        compiler_params=TINY,
        cost_estimate=pl.CostEstimate(
            flops=2 * 7 * 512 * 512 * 128, bytes_accessed=3 << 19, transcendentals=0
        ),
        name=f"taylor{step}",
    )(prop, walker, one_body)


def gather_fields(fields):
    spread = jnp.broadcast_to(fields[None], (16,) + fields.shape)
    every = lax.all_to_all(spread, "wide", split_axis=0, concat_axis=0, tiled=True)
    return every.reshape(256, 256)


def local(cholesky, fields, walkers, one_body):
    me = lax.axis_index("narrow").astype(jnp.int32).reshape(1)
    fields_all = gather_fields(fields)
    steps = (0, 1)
    cholesky = pltpu.with_memory_space_constraint(cholesky, pltpu.HBM)
    made = [partials(p, me, fields_all, cholesky) for p in range(3)]
    keep = {s: [made[p][s] for p in range(3)] for s in steps}
    sent = {s: [swap(made[p][2 + s], ORDERS[p][0]) for p in range(3)] for s in steps}
    for stage, rows in ((1, 32), (2, 16)):
        for s in steps:
            if s == 1:
                sent[1], send = lax.optimization_barrier((sent[1], send))
            sum_of = lambda half: [plus(keep[s][p][half], sent[s][p][half]) for p in range(3)]
            send, kept = sum_of(slice(rows, None)), sum_of(slice(0, rows))
            sent[s] = [swap(send[p], ORDERS[p][stage]) for p in range(3)]
            keep[s] = kept
    current = walkers.reshape(512, 128)
    for s in steps:
        tiles = owner_tiles(s, list(zip(keep[s], sent[s])))
        prop = lax.all_to_all(tiles, "wide", split_axis=0, concat_axis=0, tiled=True)
        current = taylor(s, prop.reshape(512, 512), current, one_body)
    return current.reshape(walkers.shape)


def solution(mesh):
    return jax.shard_map(
        local,
        mesh=mesh,
        in_specs=(
            P("narrow", "wide"),
            P(None, "wide", "narrow"),
            P(("wide", "narrow"), None, None),
            P(),
        ),
        out_specs=P(("wide", "narrow"), None, None),
        check_vma=False,
    )
```
